32 devices in a mesh: dp: 2 (over x), fsdp: 16 (over z, y, core).
Axes of the slice: x: 2, y: 2, z: 4, core: 2. Of those that a mesh axis runs over, the one named last changes fastest.
Arguments:
- tokens: bfloat16 [32, 1024, 768], P(('dp', 'fsdp')), may hold values from -6 to 6
- segments: int32 [32, 1024], P(('dp', 'fsdp')), may hold values from -1 to 12, as said below
- thresholds: float32 [32], P(('dp', 'fsdp')), may hold values from 0.25 to 6
- qkv_weight: bfloat16 [768, 2304], P(('dp', 'fsdp')), may hold values from -0.21650635 to 0.21650635
- out_weight: bfloat16 [768, 768], P(('dp', 'fsdp')), may hold values from -0.4375 to 0.4375
- up_weight: bfloat16 [768, 3072], P(('dp', 'fsdp')), may hold values from -0.21875 to 0.21875
- down_weight: bfloat16 [3072, 768], P(('dp', 'fsdp')), may hold values from -0.109375 to 0.109375
- attn_gain: bfloat16 [768], P(('dp', 'fsdp')), may hold values from 0.5 to 1.5
- attn_shift: bfloat16 [768], P(('dp', 'fsdp')), may hold values from -1.1953125 to 1.1953125
- mlp_gain: bfloat16 [768], P(('dp', 'fsdp')), may hold values from 0.5 to 1.5
- mlp_shift: bfloat16 [768], P(('dp', 'fsdp')), may hold values from -1.1953125 to 1.1953125
- cotangent: bfloat16 [32, 1024, 768], P(('dp', 'fsdp')), may hold values from -6 to 6
Outputs:
- output: bfloat16 [32, 1024, 768], P(('dp', 'fsdp'))
- grad_tokens: float32 [32, 1024, 768], P(('dp', 'fsdp'))
- grad_qkv: float32 [768, 2304], P(('dp', 'fsdp'))
- grad_out: float32 [768, 768], P(('dp', 'fsdp'))
- grad_up: float32 [768, 3072], P(('dp', 'fsdp'))
- grad_down: float32 [3072, 768], P(('dp', 'fsdp'))
- grad_attn_gain: float32 [768], P(('dp', 'fsdp'))
- grad_attn_shift: float32 [768], P(('dp', 'fsdp'))
- grad_mlp_gain: float32 [768], P(('dp', 'fsdp'))
- grad_mlp_shift: float32 [768], P(('dp', 'fsdp'))
- fraction: float32 [], replicated
The draws below stay inside these ranges and needn't reach their ends.
Inputs may be any that keep to these rules, and one draw needn't show every extreme that they name: `segments`: in each packed row the document numbers start at 0 and never fall; every document has 1 to 256 tokens and one document of exactly 256 tokens lies in every row; each row ends in 1 to 255 padding tokens marked -1.
All inputs are finite; a program needn't handle non-finite values.
Results may differ from the reference program's by a relative error of at most 0.011.
The reference program's roundings to bfloat16 on the way count: a program that leaves them out, or rounds other values in their place, can miss the bound.
Values may be sent and summed in bfloat16 or wider, within the bound.
No kernel may reach another device: no remote copies, remote signals or barrier semaphores. Data moves between devices by JAX's collectives and lax.ppermute only.
A program may use at most 256 MiB of HBM per device.

```python
import math
import jax
import jax.numpy as jnp
from jax import lax

D = 768
HEADS = 12
HD = 64
FF = 3072
LEN = 1024
DOC = 256
ROWS = 32
NDOC = 16


def draw_segments(key, part):
    first_key, second_key, third_key = jax.random.split(jax.random.fold_in(key, 17), 3)
    slots = jnp.arange(NDOC)[None, :]
    row_ids = jnp.arange(ROWS)[:, None]
    lengths = jax.random.randint(first_key, (ROWS, NDOC), DOC // 4, DOC + 1)
    chosen = jax.random.randint(second_key, (ROWS, 1), 0, 3)
    chosen = jnp.where(row_ids == 0, 0, chosen)
    lengths = jnp.where(row_ids == 0, DOC // 4, lengths)
    lengths = jnp.where(slots == chosen, DOC, lengths)
    ends = jnp.cumsum(lengths, axis=1)
    places = jnp.arange(LEN)
    numbers = jnp.sum((ends[:, None, :] <= places[None, :, None]).astype(jnp.int32), axis=2)
    padding = jax.random.randint(third_key, (ROWS, 1), 1, DOC)
    padding = jnp.where(row_ids == 0, 1, padding)
    numbers = jnp.where(places[None, :] >= LEN - padding, -1, numbers)
    return numbers.astype(jnp.int32)


def draw_qkv_weight(key, part):
    base_key = jax.random.fold_in(key, 29)
    values = jnp.clip(jax.random.normal(base_key, (D, 3 * D), jnp.float32), -6.0, 6.0)
    columns = jnp.arange(3 * D)[None, :]
    factor = jnp.where(columns < HD, 0.05, 1.0)
    return (values * factor * D ** (-0.5)).astype(jnp.bfloat16)


def block_levels(key, shape, shards, least, high):
    def one(position, blocks):
        draws = jax.random.uniform(jax.random.fold_in(jax.random.fold_in(key, 6), position), (blocks,), jnp.float32, least / len(shards), high / len(shards))
        return jnp.repeat(jnp.exp(draws), shape[position] // blocks).reshape((-1,) + (1,) * (len(shape) - position - 1))

    loudness = one(*shards[0])
    for cut in shards[1:]:
        loudness = loudness * one(*cut)
    return loudness


def centred(rng, dims, scale, most, cuts=(), kind=jnp.bfloat16):
    drawn = scale * jax.random.normal(rng, dims, jnp.float32)
    if cuts:
        drawn = drawn * block_levels(rng, dims, cuts, -0.22, 0.18)
    return jnp.clip(drawn, -most, most).astype(kind)


def setup_inputs(seed: int = 0) -> dict:
    keys = jax.random.split(jax.random.key(seed), 13)
    return {
        "tokens": centred(keys[0], (ROWS, LEN, D), 1.0, 6.0, ((0, 32),)),
        "segments": draw_segments(jax.random.fold_in(keys[12], 71), 0),
        "thresholds": jnp.clip(jnp.exp(math.log(6.0) - 3.1780538 * jax.random.uniform(keys[2], (ROWS,), jnp.float32) ** block_levels(keys[2], (ROWS,), ((0, 32),), -0.2, 0.2)), 0.25, 6.0),
        "qkv_weight": draw_qkv_weight(jax.random.fold_in(keys[12], 71), 0),
        "out_weight": centred(keys[4], (D, D), (D // 4) ** -0.5, 0.4375, ((0, 32),)),
        "up_weight": centred(keys[5], (D, FF), D ** -0.5, 0.21875, ((0, 32),)),
        "down_weight": centred(keys[6], (FF, D), FF ** -0.5, 0.109375, ((0, 32),)),
        "attn_gain": jnp.clip(1.0 + 0.1 * jax.random.normal(keys[7], (D,), jnp.float32), 0.5, 1.5).astype(jnp.bfloat16),
        "attn_shift": centred(keys[8], (D,), 0.2, 1.1953125, ((0, 32),)),
        "mlp_gain": jnp.clip(1.0 + 0.1 * jax.random.normal(keys[9], (D,), jnp.float32), 0.5, 1.5).astype(jnp.bfloat16),
        "mlp_shift": centred(keys[10], (D,), 0.2, 1.1953125, ((0, 32),)),
        "cotangent": centred(keys[11], (ROWS, LEN, D), 1.0, 6.0, ((0, 32),)),
    }


@jax.custom_vjp
def low(v):
    return lax.optimization_barrier(v.astype(jnp.bfloat16)).astype(jnp.float32)

@jax.custom_vjp
def low_back(v):
    return v

def low_keep(v):
    return (low(v), None)

def low_pass(kept, grad):
    return (grad,)

def back_keep(v):
    return (v, None)

def back_low(kept, grad):
    return (low(grad),)
low.defvjp(low_keep, low_pass)
low_back.defvjp(back_keep, back_low)
EPSILON = 1e-05
HIGHEST = lax.Precision.HIGHEST
NEGATIVE = -1e+30
SOFT_WIDTH = 0.25

def layer_norm(values, gain, shift):
    center = values - lax.optimization_barrier(jnp.mean(values, axis=-1, keepdims=True))
    spread = lax.optimization_barrier(jnp.mean(center * center, axis=-1, keepdims=True))
    return center * lax.rsqrt(spread + EPSILON) * gain + shift

def pair_masks(seg_row):
    places = jnp.arange(LEN)
    same = seg_row[:, None] == seg_row[None, :]
    earlier = places[None, :] < places[:, None]
    key_live = seg_row[None, :] >= 0
    strict = same & earlier & key_live
    allowed = strict | (places[:, None] == places[None, :])
    return (allowed, strict)

def shifted_sum(select):
    running = jnp.cumsum(select, axis=0)
    return jnp.concatenate([jnp.zeros((1, LEN), running.dtype), running[:-1]], axis=0)

def layer_row(params, row, seg_row, limit):
    qkv_weight, out_weight, up_weight, down_weight, attn_gain, attn_shift, mlp_gain, mlp_shift = params
    allowed, strict = pair_masks(seg_row)
    normed = low(layer_norm(row, attn_gain, attn_shift))
    project = low_back(low(jnp.dot(normed, qkv_weight, precision=HIGHEST)))
    parts = project.reshape(LEN, 3, HEADS, HD)
    queries = parts[:, 0]
    keys_all = parts[:, 1]
    values_all = parts[:, 2]
    scores = low_back(jnp.einsum('qhd,khd->hqk', queries, keys_all, precision=HIGHEST) * HD ** (-0.5))
    select = jnp.where(strict, jnp.maximum(scores[0], 0.0), 0.0)
    selsum = shifted_sum(select)
    logits = jnp.where(allowed[None], scores - selsum[None], NEGATIVE)
    top = lax.optimization_barrier(jnp.max(logits, axis=-1, keepdims=True))
    expo = jnp.exp(logits - top)
    probs = expo / lax.optimization_barrier(jnp.sum(expo, axis=-1, keepdims=True))
    mixed = jnp.einsum('hqk,khd->qhd', low(probs), values_all, precision=HIGHEST).reshape(LEN, D)
    mixed = low_back(low(mixed))
    branch = low_back(jnp.dot(mixed, out_weight, precision=HIGHEST))
    middle = row + branch
    normed_two = low(layer_norm(middle, mlp_gain, mlp_shift))
    hidden = low_back(jnp.dot(normed_two, up_weight, precision=HIGHEST))
    active = low(jax.nn.gelu(hidden, approximate=True))
    result = middle + jnp.dot(active, down_weight, precision=HIGHEST)
    soft = jnp.sum(jnp.where(strict, jax.nn.sigmoid((selsum - limit) / SOFT_WIDTH), 0.0))
    pairs = jnp.sum(strict.astype(result.dtype))
    return (result, (soft, pairs))

def reference(tokens, segments, thresholds, qkv_weight, out_weight, up_weight, down_weight, attn_gain, attn_shift, mlp_gain, mlp_shift, cotangent):
    params = tuple((weight.astype(jnp.float32) for weight in (qkv_weight, out_weight, up_weight, down_weight, attn_gain, attn_shift, mlp_gain, mlp_shift)))
    inputs = tokens.astype(jnp.float32)
    live = (segments >= 0).astype(jnp.float32)
    seed_grad = cotangent.astype(jnp.float32) * live[:, :, None]

    def forward(weights, rows_in):

        def one_row(item):
            row, seg_row, limit = item
            return jax.checkpoint(layer_row)(weights, row, seg_row, limit)
        results, stats = lax.map(one_row, (rows_in, segments, thresholds))
        return (results, stats)
    results, pull, stats = jax.vjp(forward, params, inputs, has_aux=True)
    grad_params, grad_inputs = pull(seed_grad)
    fraction = jnp.sum(stats[0]) / jnp.sum(stats[1])
    return (results.astype(jnp.bfloat16), grad_inputs, grad_params[0], grad_params[1], grad_params[2], grad_params[3], grad_params[4], grad_params[5], grad_params[6], grad_params[7], fraction)
```

```python
import functools

import jax
import jax.numpy as jnp
from jax import lax
from jax.experimental import pallas as pl
from jax.experimental.pallas import tpu as pltpu
from jax.sharding import PartitionSpec as P

HEADS = 12
HD = 64


EPSILON = 1e-05
NEGATIVE = -1e30
SOFT_WIDTH = 0.25


def norm_forward(values, gain, shift):
    center = values - jnp.mean(values, axis=-1, keepdims=True)
    spread = jnp.mean(center * center, axis=-1, keepdims=True)
    inverse = lax.rsqrt(spread + EPSILON)
    unit = center * inverse
    return (unit * gain + shift, unit, inverse)


def norm_backward(grad_normed, unit, inverse, gain):
    grad_unit = grad_normed * gain
    grad_gain = jnp.sum(grad_normed * unit, axis=0)
    grad_shift = jnp.sum(grad_normed, axis=0)
    centered = grad_unit - jnp.mean(grad_unit, axis=-1, keepdims=True)
    grad_input = inverse * (centered - unit * jnp.mean(grad_unit * unit, axis=-1, keepdims=True))
    return (grad_input, grad_gain, grad_shift)


BLOCK = 128
SPAN = 384
NT = (((1,), (1,)), ((), ()))
TN = (((0,), (0,)), ((), ()))


def dot_nt(a, b):
    return lax.dot_general(a, b, NT, preferred_element_type=jnp.float32)


def dot_tn(a, b):
    return lax.dot_general(a, b, TN, preferred_element_type=jnp.float32)


def halves(pair):
    lane = lax.broadcasted_iota(jnp.int32, pair.shape, 1)
    zero = jnp.zeros_like(pair)
    return (jnp.where(lane < HD, pair, zero), jnp.where(lane < HD, zero, pair))


def attend_kernel(limit_ref, seg_ref, project_ref, mixed_ref, lse_ref, bias_ref, stat_ref, column_ref):
    block = pl.program_id(0)
    width = HEADS * HD
    here = pl.multiple_of(block * BLOCK, BLOCK)
    first_key = pl.multiple_of(jnp.maximum(block - 2, 0) * BLOCK, BLOCK)
    rows = pl.ds(here, BLOCK)
    span = pl.ds(first_key, SPAN)

    @pl.when(block == 0)
    def _():
        column_ref[...] = jnp.zeros_like(column_ref)
        stat_ref[...] = jnp.zeros_like(stat_ref)

    low_lane = lax.broadcasted_iota(jnp.int32, (BLOCK, BLOCK), 1)
    bias = None
    for pair in range(HEADS // 2):
        at = pair * 2 * HD
        lanes = slice(at, at + 2 * HD)
        queries = halves(project_ref[rows, lanes] * jnp.bfloat16(HD ** (-0.5)))
        key = project_ref[span, width + at : width + at + 2 * HD]
        value = project_ref[span, 2 * width + at : 2 * width + at + 2 * HD]
        both = dot_nt(key, jnp.concatenate(queries, axis=0))
        outs = []
        for side in range(2):
            head = 2 * pair + side
            scores = both[:, side * BLOCK : (side + 1) * BLOCK]
            if bias is None:
                seg_key = jnp.broadcast_to(seg_ref[:, span], (BLOCK, SPAN)).T
                key_at = first_key + lax.broadcasted_iota(jnp.int32, (SPAN, BLOCK), 0)
                query_at = here + lax.broadcasted_iota(jnp.int32, (SPAN, BLOCK), 1)
                strict = (key_at < query_at) & (seg_ref[:, rows] == seg_key) & (seg_key >= 0)
                allowed = strict | (key_at == query_at)
                select = jnp.where(strict, jnp.maximum(scores, 0.0), 0.0)
                at_row = lax.broadcasted_iota(jnp.int32, (BLOCK, 2 * BLOCK), 0)
                at_lane = lax.broadcasted_iota(jnp.int32, (BLOCK, 2 * BLOCK), 1)
                sums = jnp.dot(
                    select,
                    ((at_row < at_lane) | (at_lane >= BLOCK)).astype(jnp.float32),
                    precision=lax.Precision.HIGHEST,
                    preferred_element_type=jnp.float32,
                )
                before = column_ref[span, :]
                selsum = before + sums[:, :BLOCK]
                column_ref[span, :] = before + sums[:, BLOCK:]
                bias = jnp.where(allowed, -selsum, NEGATIVE)
                bias_ref[...] = bias
                offset = (selsum - limit_ref[0]) * (1.0 / SOFT_WIDTH)
                soft = jnp.where(strict, 1.0 / (1.0 + jnp.exp(-offset)), 0.0)
                stat_ref[0:1, :] += jnp.sum(soft, axis=0, keepdims=True)
                stat_ref[1:2, :] += jnp.sum(jnp.where(strict, 1.0, 0.0), axis=0, keepdims=True)
            logits = scores + bias
            top = jnp.max(logits, axis=0, keepdims=True)
            expo = jnp.exp(logits - top)
            total = jnp.sum(expo, axis=0, keepdims=True)
            probs = (expo * (1.0 / total)).astype(jnp.bfloat16)
            outs.append(dot_tn(probs, value))
            lse_ref[head : head + 1, :] = top + jnp.log(total)
        mixed_ref[:, lanes] = jnp.where(low_lane < HD, outs[0], outs[1]).astype(jnp.bfloat16)


def attend_row(project_row, seg_row, limit):
    length = seg_row.shape[0]
    width = HEADS * HD
    blocks = length // BLOCK
    return pl.pallas_call(
        attend_kernel,
        name="attend_forward",
        grid=(blocks,),
        in_specs=[
            pl.BlockSpec(memory_space=pltpu.SMEM),
            pl.BlockSpec((1, length), lambda i: (0, 0)),
            pl.BlockSpec((length, 3 * width), lambda i: (0, 0), pipeline_mode=pl.Buffered(1)),
        ],
        out_specs=[
            pl.BlockSpec((BLOCK, width), lambda i: (i, 0)),
            pl.BlockSpec((16, BLOCK), lambda i: (0, i)),
            pl.BlockSpec((None, SPAN, BLOCK), lambda i: (i, 0, 0)),
            pl.BlockSpec((8, BLOCK), lambda i: (0, 0)),
        ],
        out_shape=[
            jax.ShapeDtypeStruct((length, width), jnp.bfloat16),
            jax.ShapeDtypeStruct((16, length), jnp.float32),
            jax.ShapeDtypeStruct((blocks, SPAN, BLOCK), jnp.float32),
            jax.ShapeDtypeStruct((8, BLOCK), jnp.float32),
        ],
        scratch_shapes=[pltpu.VMEM((length, BLOCK), jnp.float32)],
        cost_estimate=pl.CostEstimate(
            flops=4 * length * SPAN * width, transcendentals=HEADS * length * SPAN, bytes_accessed=10 * length * width
        ),
    )(limit, seg_row[None], project_row)


def attend_back_kernel(
    project_ref, grad_ref, lse_ref, bias_ref, out_ref, key_ref, value_ref, column_ref, select_ref
):
    block = pl.num_programs(0) - 1 - pl.program_id(0)
    width = HEADS * HD
    here = pl.multiple_of(block * BLOCK, BLOCK)
    first_key = pl.multiple_of(jnp.maximum(block - 2, 0) * BLOCK, BLOCK)
    rows = pl.ds(here, BLOCK)
    span = pl.ds(first_key, SPAN)

    @pl.when(pl.program_id(0) == 0)
    def _():
        key_ref[...] = jnp.zeros_like(key_ref)
        value_ref[...] = jnp.zeros_like(value_ref)
        column_ref[...] = jnp.zeros_like(column_ref)

    bias = jnp.concatenate([bias_ref[...], bias_ref[...]], axis=1)
    for pair in reversed(range(HEADS // 2)):
        at = pair * 2 * HD
        lanes = slice(at, at + 2 * HD)
        queries = halves(project_ref[rows, lanes] * jnp.bfloat16(HD ** (-0.5)))
        queries = jnp.concatenate(queries, axis=0)
        key = project_ref[span, width + at : width + at + 2 * HD]
        value = project_ref[span, 2 * width + at : 2 * width + at + 2 * HD]
        grads = jnp.concatenate(halves(grad_ref[:, lanes]), axis=0)
        lse = jnp.concatenate(
            [lse_ref[2 * pair : 2 * pair + 1, :], lse_ref[2 * pair + 1 : 2 * pair + 2, :]], axis=1
        )
        scores = dot_nt(key, queries)
        probs = jnp.exp(scores + bias - lse)
        grad_probs = dot_nt(value, grads)
        inner = jnp.sum(probs * grad_probs, axis=0, keepdims=True)
        logits_grads = probs * (grad_probs - inner)
        both = logits_grads[:, :BLOCK] + logits_grads[:, BLOCK:]
        if pair == HEADS // 2 - 1:
            select_ref[...] = -both
        else:
            select_ref[...] -= both
        if pair == 0:
            grad_selsum = select_ref[...]
            at_row = lax.broadcasted_iota(jnp.int32, (BLOCK, 2 * BLOCK), 0)
            at_lane = lax.broadcasted_iota(jnp.int32, (BLOCK, 2 * BLOCK), 1)
            after = ((at_row > at_lane) | (at_lane >= BLOCK)).astype(jnp.float32)
            sums = jnp.dot(
                grad_selsum,
                after,
                precision=lax.Precision.HIGHEST,
                preferred_element_type=jnp.float32,
            )
            later = column_ref[span, :]
            grad_select = later + sums[:, :BLOCK]
            column_ref[span, :] = later + sums[:, BLOCK:]
            key_at = first_key + lax.broadcasted_iota(jnp.int32, (SPAN, BLOCK), 0)
            query_at = here + lax.broadcasted_iota(jnp.int32, (SPAN, BLOCK), 1)
            chosen = (bias[:, :BLOCK] > 0.5 * NEGATIVE) & (key_at != query_at)
            chosen = chosen & (scores[:, :BLOCK] > 0.0)
            grad_select = jnp.where(chosen, grad_select, 0.0)
            logits_grads = jnp.concatenate(
                [logits_grads[:, :BLOCK] + grad_select, logits_grads[:, BLOCK:]], axis=1
            )
        low_grads = logits_grads.astype(jnp.bfloat16)
        value_ref[span, lanes] += jnp.dot(
            probs.astype(jnp.bfloat16), grads, preferred_element_type=jnp.float32
        )
        key_ref[span, lanes] += jnp.dot(low_grads, queries, preferred_element_type=jnp.float32)
        query_grad = jnp.dot(key.T, low_grads, preferred_element_type=jnp.float32)
        query_grad = jnp.concatenate([query_grad[:HD, :BLOCK], query_grad[HD:, BLOCK:]], axis=0)
        out_ref[:, lanes] = (query_grad.T * HD ** (-0.5)).astype(jnp.bfloat16)
    out_ref[:, width : 2 * width] = key_ref[rows, :].astype(jnp.bfloat16)
    out_ref[:, 2 * width :] = value_ref[rows, :].astype(jnp.bfloat16)


def row_back(project_row, grad_row, lse_row, bias_row):
    length = project_row.shape[0]
    width = HEADS * HD
    blocks = length // BLOCK
    return pl.pallas_call(
        attend_back_kernel,
        name="attend_backward",
        grid=(blocks,),
        in_specs=[
            pl.BlockSpec((length, 3 * width), lambda i: (0, 0), pipeline_mode=pl.Buffered(1)),
            pl.BlockSpec((BLOCK, width), lambda i: (blocks - 1 - i, 0)),
            pl.BlockSpec((16, BLOCK), lambda i: (0, blocks - 1 - i)),
            pl.BlockSpec((None, SPAN, BLOCK), lambda i: (blocks - 1 - i, 0, 0)),
        ],
        out_specs=pl.BlockSpec((BLOCK, 3 * width), lambda i: (blocks - 1 - i, 0)),
        out_shape=jax.ShapeDtypeStruct((length, 3 * width), jnp.bfloat16),
        scratch_shapes=[
            pltpu.VMEM((length, width), jnp.float32),
            pltpu.VMEM((length, width), jnp.float32),
            pltpu.VMEM((length, BLOCK), jnp.float32),
            pltpu.VMEM((SPAN, BLOCK), jnp.float32),
        ],
        cost_estimate=pl.CostEstimate(
            flops=10 * length * SPAN * width, transcendentals=HEADS * length * SPAN, bytes_accessed=14 * length * width
        ),
    )(project_row, grad_row, lse_row, bias_row)


BOTH = ("dp", "fsdp")


def bit_count(sizes):
    return (sizes["dp"] * sizes["fsdp"]).bit_length() - 1


def my_bits(sizes):
    count = bit_count(sizes)
    number = lax.axis_index("dp") * sizes["fsdp"] + lax.axis_index("fsdp")
    return [(number >> (count - 1 - place)) & 1 for place in range(count)]


def exchange(value, sizes, places):
    count = bit_count(sizes)
    masks = [1 << (count - 1 - place) for place in places]
    return lax.ppermute(value, BOTH, [(i, i ^ masks[i & 1]) for i in range(2**count)])


def side_of(shape, axis):
    return lax.broadcasted_iota(jnp.int32, shape, axis)


def join(mine, other, at, bit):
    shape = mine.shape[:at] + (2,) + mine.shape[at:]
    return jnp.where(side_of(shape, at) == bit, jnp.expand_dims(mine, at), jnp.expand_dims(other, at))


def gather_far(shard, sizes):
    bits = my_bits(sizes)
    value = shard
    for place in range(1, len(bits) - 2):
        value = join(value, exchange(value, sizes, (place, place)), place - 1, bits[place])
    return value


def gather_near(value, sizes):
    bits = my_bits(sizes)
    near = len(bits) - 2
    other = exchange(value, sizes, (0, near))
    return join(value, other, 0, jnp.where(bits[-1] == 0, bits[0], bits[near]))


def gather_next(value, sizes):
    bits = my_bits(sizes)
    near = len(bits) - 2
    other = exchange(value, sizes, (near, 0))
    by_first = join(value, other, near, bits[near])
    by_near = join(jnp.moveaxis(value, 0, near - 1), jnp.moveaxis(other, 0, near - 1), 0, bits[0])
    return jnp.where(bits[-1] == 0, by_first, by_near)


def gather_core(value, sizes):
    bits = my_bits(sizes)
    last = len(bits) - 1
    value = join(value, exchange(value, sizes, (last, last)), last, bits[last])
    return value.reshape((-1,) + value.shape[last + 2 :])


def pick(value, at, bit):
    return lax.dynamic_index_in_dim(value, bit, at, keepdims=False)


def add_exchange(mine, sent, sizes, places, kind):
    return mine.astype(jnp.float32) + exchange(sent.astype(kind), sizes, places).astype(jnp.float32)


def scatter_core(partial, sizes, kind=jnp.bfloat16):
    bits = my_bits(sizes)
    last = len(bits) - 1
    shape = (2,) * len(bits) + (partial.shape[0] >> len(bits),) + partial.shape[1:]
    view = partial.reshape(shape)
    return add_exchange(
        pick(view, last, bits[last]), pick(view, last, 1 - bits[last]), sizes, (last, last), kind
    )


def scatter_near(value, sizes, kind=jnp.bfloat16):
    bits = my_bits(sizes)
    near = len(bits) - 2
    even = bits[-1] == 0

    def cut(flip):
        by_near = pick(value, near, bits[near] ^ flip)
        by_first = jnp.moveaxis(pick(value, 0, bits[0] ^ flip), near - 1, 0)
        return jnp.where(even, by_near, by_first)

    return add_exchange(cut(0), cut(1), sizes, (near, 0), kind)


def scatter_next(value, sizes, kind=jnp.bfloat16):
    bits = my_bits(sizes)
    near = len(bits) - 2
    side = jnp.where(bits[-1] == 0, bits[0], bits[near])
    return add_exchange(pick(value, 0, side), pick(value, 0, 1 - side), sizes, (0, near), kind)


def scatter_far(value, sizes, kind=jnp.bfloat16):
    bits = my_bits(sizes)
    for place in reversed(range(1, len(bits) - 2)):
        value = add_exchange(
            pick(value, place - 1, bits[place]),
            pick(value, place - 1, 1 - bits[place]),
            sizes,
            (place, place),
            kind,
        )
    return value


def tie(*values):
    return lax.optimization_barrier(values)


def body(
    sizes,
    tokens,
    segments,
    thresholds,
    qkv_weight,
    out_weight,
    up_weight,
    down_weight,
    attn_gain,
    attn_shift,
    mlp_gain,
    mlp_shift,
    cotangent,
):
    rows_here, length, width = tokens.shape
    shards = sizes["dp"] * sizes["fsdp"]
    piece = width // shards
    small = jnp.stack([attn_gain, attn_shift, mlp_gain, mlp_shift], axis=1)
    small = jnp.pad(small, ((0, 0), (0, 128 - 4)))
    wide = up_weight.shape[1]
    second = lax.all_gather(
        jnp.concatenate([up_weight, out_weight], axis=1), BOTH, axis=0, tiled=True
    )
    up_full, out_full = (second[:, :wide], second[:, wide:])
    first = gather_far(jnp.concatenate([qkv_weight, small], axis=1), sizes)
    first, down_weight = tie(first, down_weight)
    down_full = gather_far(down_weight, sizes)
    first = gather_next(gather_near(first, sizes), sizes)
    first, down_full = tie(first, down_full)
    first = gather_core(first, sizes)
    down_full = gather_near(down_full, sizes)
    qkv_full = first[:, : 3 * width]
    small = first[:, 3 * width : 3 * width + 4].astype(jnp.float32).T
    gain_one, shift_one, gain_two, shift_two = (small[0], small[1], small[2], small[3])
    flat = tokens.astype(jnp.float32).reshape(rows_here * length, width)
    normed_float, unit_one, inverse_one = norm_forward(flat, gain_one, shift_one)
    normed = normed_float.astype(jnp.bfloat16)
    project = jnp.dot(normed, qkv_full, preferred_element_type=jnp.float32).astype(jnp.bfloat16)
    project, down_full = tie(project, down_full)
    down_full = gather_next(down_full, sizes)
    project_rows = project.reshape(rows_here, length, 3 * width)
    forward = [
        attend_row(project_rows[row], segments[row], thresholds[row : row + 1])
        for row in range(rows_here)
    ]
    mixed_flat = jnp.concatenate([item[0] for item in forward], axis=0)
    soft = sum(jnp.sum(item[3][0]) for item in forward)
    pairs = sum(jnp.sum(item[3][1]) for item in forward)
    middle = flat + jnp.dot(mixed_flat, out_full, preferred_element_type=jnp.float32)
    normed_two_float, unit_two, inverse_two = norm_forward(middle, gain_two, shift_two)
    normed_two, down_full = tie(normed_two_float.astype(jnp.bfloat16), down_full)
    down_full = gather_core(down_full, sizes)
    hidden = jnp.dot(normed_two, up_full, preferred_element_type=jnp.float32)
    active = jax.nn.gelu(hidden, approximate=True).astype(jnp.bfloat16)
    grad_seed = jnp.where(
        (segments >= 0)[:, :, None], cotangent, jnp.zeros_like(cotangent)
    ).reshape(rows_here * length, width)
    grad_down = jnp.dot(active.T, grad_seed, preferred_element_type=jnp.float32)
    down_full, grad_down = tie(down_full, grad_down)
    grad_down = lax.psum_scatter(
        grad_down.astype(jnp.bfloat16), BOTH, scatter_dimension=0, tiled=True
    ).astype(jnp.float32)
    grad_active = jnp.dot(grad_seed, down_full.T, preferred_element_type=jnp.float32)
    unused_value, gelu_pull = jax.vjp(lambda values: jax.nn.gelu(values, approximate=True), hidden)
    grad_hidden = gelu_pull(grad_active)[0].astype(jnp.bfloat16)
    grad_up = jnp.dot(normed_two.T, grad_hidden, preferred_element_type=jnp.float32)
    grad_hidden, grad_up = tie(grad_hidden, grad_up.astype(jnp.bfloat16))
    grad_up = scatter_core(grad_up, sizes)
    grad_normed_two = jnp.dot(grad_hidden, up_full.T, preferred_element_type=jnp.float32)
    grad_middle_part, grad_gain_two, grad_shift_two = norm_backward(
        grad_normed_two, unit_two, inverse_two, gain_two
    )
    grad_middle = grad_seed.astype(jnp.float32) + grad_middle_part
    grad_branch = grad_middle.astype(jnp.bfloat16)
    grad_out = jnp.dot(mixed_flat.T, grad_branch, preferred_element_type=jnp.float32)
    grad_branch, grad_out, grad_up = tie(grad_branch, grad_out.astype(jnp.bfloat16), grad_up)
    grad_up = scatter_near(grad_up, sizes)
    grad_out = scatter_core(grad_out, sizes)
    grad_mixed = jnp.dot(grad_branch, out_full.T, preferred_element_type=jnp.float32).astype(
        jnp.bfloat16
    )
    grad_mixed, grad_out = tie(grad_mixed.reshape(rows_here, length, width), grad_out)
    grad_out = scatter_near(grad_out, sizes)
    grad_project = jnp.concatenate(
        [
            row_back(project_rows[row], grad_mixed[row], forward[row][1], forward[row][2])
            for row in range(rows_here)
        ],
        axis=0,
    )
    grad_project, grad_up, grad_out = tie(grad_project, grad_up, grad_out)
    upper = scatter_next(jnp.concatenate([grad_up, grad_out], axis=-1), sizes)
    grad_qkv = jnp.dot(normed.T, grad_project, preferred_element_type=jnp.float32)
    grad_qkv, active = tie(grad_qkv.astype(jnp.bfloat16), active)
    grad_qkv = scatter_core(grad_qkv, sizes)
    result = middle + jnp.dot(active, down_full, preferred_element_type=jnp.float32)
    output = result.astype(jnp.bfloat16).reshape(rows_here, length, width)
    grad_project, grad_qkv, output = tie(grad_project, grad_qkv, output)
    upper = scatter_far(upper, sizes)
    grad_up, grad_out = (upper[:, :wide], upper[:, wide:])
    grad_qkv = scatter_far(scatter_next(scatter_near(grad_qkv, sizes), sizes), sizes)
    grad_normed = jnp.dot(grad_project, qkv_full.T, preferred_element_type=jnp.float32)
    grad_input_part, grad_gain_one, grad_shift_one = norm_backward(
        grad_normed, unit_one, inverse_one, gain_one
    )
    grad_tokens = (grad_middle + grad_input_part).reshape(rows_here, length, width)
    small = jnp.stack([grad_gain_one, grad_shift_one, grad_gain_two, grad_shift_two])
    small = small.reshape(4, shards, piece).transpose(1, 0, 2).reshape(shards, 4 * piece)
    totals = jnp.broadcast_to(jnp.stack([soft, pairs]), (shards, 2))
    small = jnp.concatenate([small, totals], axis=1)
    small = jnp.pad(small, ((0, 0), (0, 128 - small.shape[1])))
    small = scatter_near(scatter_core(small, sizes, jnp.float32), sizes, jnp.float32)
    small = scatter_far(scatter_next(small, sizes, jnp.float32), sizes, jnp.float32)[0]
    fraction = small[4 * piece] / small[4 * piece + 1]
    return (
        output,
        grad_tokens,
        grad_qkv,
        grad_out,
        grad_up,
        grad_down,
        small[:piece],
        small[piece : 2 * piece],
        small[2 * piece : 3 * piece],
        small[3 * piece : 4 * piece],
        fraction,
    )


def solution(mesh):
    in_specs = (
        P(("dp", "fsdp"), None, None),
        P(("dp", "fsdp"), None),
        P(("dp", "fsdp")),
        P(("dp", "fsdp"), None),
        P(("dp", "fsdp"), None),
        P(("dp", "fsdp"), None),
        P(("dp", "fsdp"), None),
        P(("dp", "fsdp")),
        P(("dp", "fsdp")),
        P(("dp", "fsdp")),
        P(("dp", "fsdp")),
        P(("dp", "fsdp"), None, None),
    )
    out_specs = (
        P(("dp", "fsdp"), None, None),
        P(("dp", "fsdp"), None, None),
        P(("dp", "fsdp"), None),
        P(("dp", "fsdp"), None),
        P(("dp", "fsdp"), None),
        P(("dp", "fsdp"), None),
        P(("dp", "fsdp")),
        P(("dp", "fsdp")),
        P(("dp", "fsdp")),
        P(("dp", "fsdp")),
        P(),
    )
    return jax.shard_map(
        functools.partial(body, dict(mesh.shape)), mesh=mesh, in_specs=in_specs, out_specs=out_specs, check_vma=False)
```

```python
import functools

import jax
import jax.numpy as jnp
from jax import lax
from jax.experimental import pallas as pl
from jax.experimental.layout import Layout, with_layout_constraint
from jax.experimental.pallas import tpu as pltpu
from jax.sharding import PartitionSpec as P

HEADS = 12
HD = 64


EPSILON = 1e-05
NEGATIVE = -1e30
SOFT_WIDTH = 0.25


def norm_forward(values, gain, shift):
    center = values - jnp.mean(values, axis=-1, keepdims=True)
    spread = jnp.mean(center * center, axis=-1, keepdims=True)
    inverse = lax.rsqrt(spread + EPSILON)
    unit = center * inverse
    return (unit * gain + shift, unit, inverse)


BLOCK = 128
SPAN = 384
NT = (((1,), (1,)), ((), ()))
TN = (((0,), (0,)), ((), ()))


def dot_nt(a, b):
    return lax.dot_general(a, b, NT, preferred_element_type=jnp.float32)


def dot_tn(a, b):
    return lax.dot_general(a, b, TN, preferred_element_type=jnp.float32)


def halves(pair):
    lane = lax.broadcasted_iota(jnp.int32, pair.shape, 1)
    zero = jnp.zeros_like(pair)
    return (jnp.where(lane < HD, pair, zero), jnp.where(lane < HD, zero, pair))


def attend_kernel(limit_ref, seg_ref, project_ref, mixed_ref, lse_ref, bias_ref, stat_ref, column_ref):
    block = pl.program_id(0)
    width = HEADS * HD
    here = pl.multiple_of(block * BLOCK, BLOCK)
    first_key = pl.multiple_of(jnp.maximum(block - 2, 0) * BLOCK, BLOCK)
    rows = pl.ds(here, BLOCK)
    span = pl.ds(first_key, SPAN)

    @pl.when(block == 0)
    def _():
        column_ref[...] = jnp.zeros_like(column_ref)
        stat_ref[...] = jnp.zeros_like(stat_ref)

    low_lane = lax.broadcasted_iota(jnp.int32, (BLOCK, BLOCK), 1)
    bias = None
    for pair in range(HEADS // 2):
        at = pair * 2 * HD
        lanes = slice(at, at + 2 * HD)
        queries = halves(project_ref[rows, lanes] * jnp.bfloat16(HD ** (-0.5)))
        key = project_ref[span, width + at : width + at + 2 * HD]
        value = project_ref[span, 2 * width + at : 2 * width + at + 2 * HD]
        both = dot_nt(key, jnp.concatenate(queries, axis=0))
        outs = []
        for side in range(2):
            head = 2 * pair + side
            scores = both[:, side * BLOCK : (side + 1) * BLOCK]
            if bias is None:
                seg_key = jnp.broadcast_to(seg_ref[:, span], (BLOCK, SPAN)).T
                key_at = first_key + lax.broadcasted_iota(jnp.int32, (SPAN, BLOCK), 0)
                query_at = here + lax.broadcasted_iota(jnp.int32, (SPAN, BLOCK), 1)
                strict = (key_at < query_at) & (seg_ref[:, rows] == seg_key) & (seg_key >= 0)
                allowed = strict | (key_at == query_at)
                select = jnp.where(strict, jnp.maximum(scores, 0.0), 0.0)
                at_row = lax.broadcasted_iota(jnp.int32, (BLOCK, 2 * BLOCK), 0)
                at_lane = lax.broadcasted_iota(jnp.int32, (BLOCK, 2 * BLOCK), 1)
                sums = jnp.dot(
                    select,
                    ((at_row < at_lane) | (at_lane >= BLOCK)).astype(jnp.float32),
                    precision=lax.Precision.HIGHEST,
                    preferred_element_type=jnp.float32,
                )
                before = column_ref[span, :]
                selsum = before + sums[:, :BLOCK]
                column_ref[span, :] = before + sums[:, BLOCK:]
                bias = jnp.where(allowed, -selsum, NEGATIVE)
                bias_ref[...] = bias
                offset = (selsum - limit_ref[0]) * (1.0 / SOFT_WIDTH)
                soft = jnp.where(strict, 1.0 / (1.0 + jnp.exp(-offset)), 0.0)
                stat_ref[0:1, :] += jnp.sum(soft, axis=0, keepdims=True)
                stat_ref[1:2, :] += jnp.sum(jnp.where(strict, 1.0, 0.0), axis=0, keepdims=True)
            logits = scores + bias
            top = jnp.max(logits, axis=0, keepdims=True)
            expo = jnp.exp(logits - top)
            total = jnp.sum(expo, axis=0, keepdims=True)
            probs = (expo * (1.0 / total)).astype(jnp.bfloat16)
            outs.append(dot_tn(probs, value))
            lse_ref[head : head + 1, :] = top + jnp.log(total)
        mixed_ref[:, lanes] = jnp.where(low_lane < HD, outs[0], outs[1]).astype(jnp.bfloat16)


def attend_row(project_row, seg_row, limit):
    length = seg_row.shape[0]
    width = HEADS * HD
    blocks = length // BLOCK
    return pl.pallas_call(
        attend_kernel,
        name="attend_forward",
        grid=(blocks,),
        in_specs=[
            pl.BlockSpec(memory_space=pltpu.SMEM),
            pl.BlockSpec((1, length), lambda i: (0, 0)),
            pl.BlockSpec((length, 3 * width), lambda i: (0, 0), pipeline_mode=pl.Buffered(1)),
        ],
        out_specs=[
            pl.BlockSpec((BLOCK, width), lambda i: (i, 0)),
            pl.BlockSpec((16, BLOCK), lambda i: (0, i)),
            pl.BlockSpec((None, SPAN, BLOCK), lambda i: (i, 0, 0)),
            pl.BlockSpec((8, BLOCK), lambda i: (0, 0)),
        ],
        out_shape=[
            jax.ShapeDtypeStruct((length, width), jnp.bfloat16),
            jax.ShapeDtypeStruct((16, length), jnp.float32),
            jax.ShapeDtypeStruct((blocks, SPAN, BLOCK), jnp.float32),
            jax.ShapeDtypeStruct((8, BLOCK), jnp.float32),
        ],
        scratch_shapes=[pltpu.VMEM((length, BLOCK), jnp.float32)],
        cost_estimate=pl.CostEstimate(
            flops=75 * length * SPAN * width, transcendentals=HEADS * length * SPAN, bytes_accessed=10 * length * width
        ),
    )(limit, seg_row[None], project_row)


def attend_back_kernel(
    project_ref, grad_ref, lse_ref, bias_ref, out_ref, key_ref, value_ref, column_ref, select_ref
):
    block = pl.num_programs(0) - 1 - pl.program_id(0)
    width = HEADS * HD
    here = pl.multiple_of(block * BLOCK, BLOCK)
    first_key = pl.multiple_of(jnp.maximum(block - 2, 0) * BLOCK, BLOCK)
    rows = pl.ds(here, BLOCK)
    span = pl.ds(first_key, SPAN)

    @pl.when(pl.program_id(0) == 0)
    def _():
        key_ref[...] = jnp.zeros_like(key_ref)
        value_ref[...] = jnp.zeros_like(value_ref)
        column_ref[...] = jnp.zeros_like(column_ref)

    bias = jnp.concatenate([bias_ref[...], bias_ref[...]], axis=1)
    for pair in reversed(range(HEADS // 2)):
        at = pair * 2 * HD
        lanes = slice(at, at + 2 * HD)
        queries = halves(project_ref[rows, lanes] * jnp.bfloat16(HD ** (-0.5)))
        queries = jnp.concatenate(queries, axis=0)
        key = project_ref[span, width + at : width + at + 2 * HD]
        value = project_ref[span, 2 * width + at : 2 * width + at + 2 * HD]
        grads = jnp.concatenate(halves(grad_ref[:, lanes]), axis=0)
        lse = jnp.concatenate(
            [lse_ref[2 * pair : 2 * pair + 1, :], lse_ref[2 * pair + 1 : 2 * pair + 2, :]], axis=1
        )
        scores = dot_nt(key, queries)
        probs = jnp.exp(scores + bias - lse)
        grad_probs = dot_nt(value, grads)
        inner = jnp.sum(probs * grad_probs, axis=0, keepdims=True)
        logits_grads = probs * (grad_probs - inner)
        both = logits_grads[:, :BLOCK] + logits_grads[:, BLOCK:]
        if pair == HEADS // 2 - 1:
            select_ref[...] = -both
        else:
            select_ref[...] -= both
        if pair == 0:
            grad_selsum = select_ref[...]
            at_row = lax.broadcasted_iota(jnp.int32, (BLOCK, 2 * BLOCK), 0)
            at_lane = lax.broadcasted_iota(jnp.int32, (BLOCK, 2 * BLOCK), 1)
            after = ((at_row > at_lane) | (at_lane >= BLOCK)).astype(jnp.float32)
            sums = jnp.dot(
                grad_selsum,
                after,
                precision=lax.Precision.HIGHEST,
                preferred_element_type=jnp.float32,
            )
            later = column_ref[span, :]
            grad_select = later + sums[:, :BLOCK]
            column_ref[span, :] = later + sums[:, BLOCK:]
            key_at = first_key + lax.broadcasted_iota(jnp.int32, (SPAN, BLOCK), 0)
            query_at = here + lax.broadcasted_iota(jnp.int32, (SPAN, BLOCK), 1)
            chosen = (bias[:, :BLOCK] > 0.5 * NEGATIVE) & (key_at != query_at)
            chosen = chosen & (scores[:, :BLOCK] > 0.0)
            grad_select = jnp.where(chosen, grad_select, 0.0)
            logits_grads = jnp.concatenate(
                [logits_grads[:, :BLOCK] + grad_select, logits_grads[:, BLOCK:]], axis=1
            )
        low_grads = logits_grads.astype(jnp.bfloat16)
        value_ref[span, lanes] += jnp.dot(
            probs.astype(jnp.bfloat16), grads, preferred_element_type=jnp.float32
        )
        key_ref[span, lanes] += jnp.dot(low_grads, queries, preferred_element_type=jnp.float32)
        query_grad = jnp.dot(key.T, low_grads, preferred_element_type=jnp.float32)
        query_grad = jnp.concatenate([query_grad[:HD, :BLOCK], query_grad[HD:, BLOCK:]], axis=0)
        out_ref[:, lanes] = (query_grad.T * HD ** (-0.5)).astype(jnp.bfloat16)
    out_ref[:, width : 2 * width] = key_ref[rows, :].astype(jnp.bfloat16)
    out_ref[:, 2 * width :] = value_ref[rows, :].astype(jnp.bfloat16)


def row_back(project_row, grad_row, lse_row, bias_row):
    length = project_row.shape[0]
    width = HEADS * HD
    blocks = length // BLOCK
    return pl.pallas_call(
        attend_back_kernel,
        name="attend_backward",
        grid=(blocks,),
        in_specs=[
            pl.BlockSpec((length, 3 * width), lambda i: (0, 0), pipeline_mode=pl.Buffered(1)),
            pl.BlockSpec((BLOCK, width), lambda i: (blocks - 1 - i, 0)),
            pl.BlockSpec((16, BLOCK), lambda i: (0, blocks - 1 - i)),
            pl.BlockSpec((None, SPAN, BLOCK), lambda i: (blocks - 1 - i, 0, 0)),
        ],
        out_specs=pl.BlockSpec((BLOCK, 3 * width), lambda i: (blocks - 1 - i, 0)),
        out_shape=jax.ShapeDtypeStruct((length, 3 * width), jnp.bfloat16),
        scratch_shapes=[
            pltpu.VMEM((length, width), jnp.float32),
            pltpu.VMEM((length, width), jnp.float32),
            pltpu.VMEM((length, BLOCK), jnp.float32),
            pltpu.VMEM((SPAN, BLOCK), jnp.float32),
        ],
        cost_estimate=pl.CostEstimate(
            flops=105 * length * SPAN * width, transcendentals=HEADS * length * SPAN, bytes_accessed=14 * length * width
        ),
    )(project_row, grad_row, lse_row, bias_row)


STRIP = 256


def norm_back_kernel(grad_ref, weight_ref, value_ref, add_ref, gain_ref, out_ref, *rest):
    sums_ref = rest[-1]

    @pl.when(pl.program_id(0) == 0)
    def _():
        sums_ref[...] = jnp.zeros_like(sums_ref)

    grad = dot_nt(grad_ref[...], weight_ref[...])
    value = value_ref[...].astype(jnp.float32)
    center = value - jnp.mean(value, axis=-1, keepdims=True)
    inverse = lax.rsqrt(jnp.mean(center * center, axis=-1, keepdims=True) + EPSILON)
    unit = center * inverse
    sums_ref[0:1, :] += jnp.sum(grad * unit, axis=0, keepdims=True)
    sums_ref[1:2, :] += jnp.sum(grad, axis=0, keepdims=True)
    grad_unit = grad * gain_ref[...]
    centered = grad_unit - jnp.mean(grad_unit, axis=-1, keepdims=True)
    back = inverse * (centered - unit * jnp.mean(grad_unit * unit, axis=-1, keepdims=True))
    total = add_ref[...].astype(jnp.float32) + back
    out_ref[...] = total
    for low_ref in rest[:-1]:
        low_ref[...] = total.astype(jnp.bfloat16)


def matmul_norm_back(name, grad, weight, value, add, gain, low):
    rows, depth = grad.shape
    width = weight.shape[0]
    strip = lambda size: pl.BlockSpec((STRIP, size), lambda i: (i, 0))
    whole = lambda *shape: pl.BlockSpec(shape, lambda i: (0, 0), pipeline_mode=pl.Buffered(1))
    return pl.pallas_call(
        norm_back_kernel,
        name=name,
        grid=(rows // STRIP,),
        in_specs=[strip(depth), whole(width, depth), strip(width), strip(width), whole(1, width)],
        out_specs=[strip(width)] * (1 + low) + [pl.BlockSpec((8, width), lambda i: (0, 0))],
        out_shape=[jax.ShapeDtypeStruct((rows, width), jnp.float32)]
        + [jax.ShapeDtypeStruct((rows, width), jnp.bfloat16)] * low
        + [jax.ShapeDtypeStruct((8, width), jnp.float32)],
        cost_estimate=pl.CostEstimate(
            flops=2 * rows * width * (depth + 3072), transcendentals=rows, bytes_accessed=2 * rows * depth + 2 * width * depth + 14 * rows * width
        ),
    )(grad, weight, value, add, gain[None])


BOTH = ("dp", "fsdp")


def bit_count(sizes):
    return (sizes["dp"] * sizes["fsdp"]).bit_length() - 1


def my_bits(sizes):
    count = bit_count(sizes)
    number = lax.axis_index("dp") * sizes["fsdp"] + lax.axis_index("fsdp")
    return [(number >> (count - 1 - place)) & 1 for place in range(count)]


def exchange(value, sizes, places):
    count = bit_count(sizes)
    masks = [1 << (count - 1 - place) for place in places]
    return lax.ppermute(value, BOTH, [(i, i ^ masks[i & 1]) for i in range(2**count)])


def side_of(shape, axis):
    return lax.broadcasted_iota(jnp.int32, shape, axis)


def join(mine, other, at, bit):
    shape = mine.shape[:at] + (2,) + mine.shape[at:]
    return jnp.where(side_of(shape, at) == bit, jnp.expand_dims(mine, at), jnp.expand_dims(other, at))


def far_places(sizes):
    return list(range(1, bit_count(sizes) - 2))


def gather_far(value, sizes, places):
    bits = my_bits(sizes)
    for place in places:
        value = join(value, exchange(value, sizes, (place, place)), place - 1, bits[place])
    return value


def gather_near(value, sizes):
    bits = my_bits(sizes)
    near = len(bits) - 2
    other = exchange(value, sizes, (0, near))
    return join(value, other, 0, jnp.where(bits[-1] == 0, bits[0], bits[near]))


def gather_last(value, beside, other, sizes):
    bits = my_bits(sizes)
    last = len(bits) - 1
    near = last - 1

    def combine(held, received, even):
        by_first = join(held, received, near, bits[near])
        by_near = join(
            jnp.moveaxis(held, 0, near - 1), jnp.moveaxis(received, 0, near - 1), 0, bits[0]
        )
        return jnp.where(even, by_first, by_near)

    even = bits[last] == 0
    other_beside = swap_core(other, sizes)
    value = join(
        combine(value, other, even), combine(beside, other_beside, jnp.logical_not(even)), last, bits[last]
    )
    return value.reshape((-1,) + value.shape[last + 2 :])


def pick(value, at, bit):
    return lax.dynamic_index_in_dim(value, bit, at, keepdims=False)


def add(mine, other):
    return mine.astype(jnp.float32) + other.astype(jnp.float32)


def core_cut(partials, sizes, flip):
    bits = my_bits(sizes)
    last = len(bits) - 1
    shape = (2,) * len(bits)
    views = [part.reshape(shape + (part.shape[0] >> len(bits),) + part.shape[1:]) for part in partials]
    return jnp.concatenate([pick(view, last, bits[last] ^ flip) for view in views], axis=-1)


def near_cut(value, sizes, flip):
    bits = my_bits(sizes)
    near = len(bits) - 2
    by_near = pick(value, near, bits[near] ^ flip)
    by_first = jnp.moveaxis(pick(value, 0, bits[0] ^ flip), near - 1, 0)
    return jnp.where(bits[-1] == 0, by_near, by_first)


def next_cut(value, sizes, flip):
    bits = my_bits(sizes)
    side = jnp.where(bits[-1] == 0, bits[0], bits[len(bits) - 2])
    return pick(value, 0, side ^ flip)


def swap_core(sent, sizes):
    last = bit_count(sizes) - 1
    return exchange(sent, sizes, (last, last))


def swap_near(sent, sizes):
    return exchange(sent, sizes, (bit_count(sizes) - 2, 0))


def swap_next(sent, sizes):
    return exchange(sent, sizes, (0, bit_count(sizes) - 2))


def far_cut(value, sizes, places, flip):
    place = places[-1]
    return pick(value, place - 1, my_bits(sizes)[place] ^ flip)


def swap_last(value, sizes):
    return exchange(value, sizes, (bit_count(sizes) - 2, 0))


def swap_far(sent, sizes, places):
    return exchange(sent, sizes, (places[-1], places[-1]))


def finish_far(value, other, sizes, places, kind=jnp.bfloat16):
    return scatter_far(add(far_cut(value, sizes, places, 0), other), sizes, places[:-1], kind)


def scatter_far(value, sizes, places, kind=jnp.bfloat16):
    bits = my_bits(sizes)
    for place in reversed(places):
        sent = pick(value, place - 1, 1 - bits[place]).astype(kind)
        value = add(pick(value, place - 1, bits[place]), exchange(sent, sizes, (place, place)))
    return value


def row_major(value):
    return with_layout_constraint(value, Layout(major_to_minor=(0, 1)))


def tie(*values):
    return lax.optimization_barrier(values)


def body(
    sizes,
    tokens,
    segments,
    thresholds,
    qkv_weight,
    out_weight,
    up_weight,
    down_weight,
    attn_gain,
    attn_shift,
    mlp_gain,
    mlp_shift,
    cotangent,
):
    rows_here, length, width = tokens.shape
    shards = sizes["dp"] * sizes["fsdp"]
    piece = width // shards
    small = jnp.stack([attn_gain, attn_shift, mlp_gain, mlp_shift], axis=1)
    small = jnp.pad(small, ((0, 0), (0, 128 - 4)))
    wide = up_weight.shape[1]
    far = far_places(sizes)
    low = jnp.bfloat16
    first = gather_far(jnp.concatenate([qkv_weight, small], axis=1), sizes, far)
    first, up_weight, out_weight = tie(first, up_weight, out_weight)
    first = gather_near(first, sizes)
    second = gather_far(jnp.concatenate([up_weight, out_weight], axis=1), sizes, far[:1])
    first, second = tie(first, second)
    other = swap_last(first, sizes)
    beside = swap_core(first, sizes)
    second = gather_far(second, sizes, far[1:])
    first = row_major(gather_last(first, beside, other, sizes))
    first, second, down_weight = tie(first, second, down_weight)
    second = gather_near(second, sizes)
    down_full = gather_far(down_weight, sizes, far[:1])
    qkv_full = first[:, : 3 * width]
    small = row_major(first[:, 3 * width :])
    small = small[:, :4].astype(jnp.float32).T
    gain_one, shift_one, gain_two, shift_two = (small[0], small[1], small[2], small[3])
    flat = tokens.astype(jnp.float32).reshape(rows_here * length, width)
    normed_float, unit_one, inverse_one = norm_forward(flat, gain_one, shift_one)
    normed = normed_float.astype(jnp.bfloat16)
    project = jnp.dot(normed, qkv_full, preferred_element_type=jnp.float32).astype(jnp.bfloat16)
    project, second, down_full = tie(project, second, down_full)
    other = swap_last(second, sizes)
    beside = swap_core(second, sizes)
    down_full = gather_far(down_full, sizes, far[1:])
    project_rows = project.reshape(rows_here, length, 3 * width)
    forward = [
        attend_row(project_rows[row], segments[row], thresholds[row : row + 1])
        for row in range(rows_here)
    ]
    mixed_flat = jnp.concatenate([item[0] for item in forward], axis=0)
    mixed_flat, other, beside, down_full = tie(mixed_flat, other, beside, down_full)
    second = row_major(gather_last(second, beside, other, sizes))
    up_full, out_full = (second[:, :wide], second[:, wide:])
    down_full = gather_near(down_full, sizes)
    soft = sum(jnp.sum(item[3][0]) for item in forward)
    pairs = sum(jnp.sum(item[3][1]) for item in forward)
    middle = flat + jnp.dot(mixed_flat, out_full, preferred_element_type=jnp.float32)
    normed_two_float, unit_two, inverse_two = norm_forward(middle, gain_two, shift_two)
    normed_two, down_full = tie(normed_two_float.astype(low), down_full)
    other = swap_last(down_full, sizes)
    beside = swap_core(down_full, sizes)
    hidden = jnp.dot(normed_two, up_full, preferred_element_type=jnp.float32)
    squared = hidden * hidden
    curve = jnp.tanh(0.7978845608 * hidden * (1.0 + 0.044715 * squared))
    active = (0.5 * hidden * (1.0 + curve)).astype(low)
    slope = 0.5 * (1.0 + curve) + hidden * (1.0 - curve * curve) * (
        0.3989422804 + 0.0535161226 * squared
    )
    slope = slope.astype(low)
    active, slope, other, beside = tie(active, slope, other, beside)
    down_full = gather_last(down_full, beside, other, sizes)
    grad_seed = jnp.where(
        (segments >= 0)[:, :, None], cotangent, jnp.zeros_like(cotangent)
    ).reshape(rows_here * length, width)
    grad_down = jnp.dot(active.T, grad_seed, preferred_element_type=jnp.float32)
    grad_down = grad_down.astype(low)
    sent, grad_seed = tie(core_cut((grad_down,), sizes, 1), grad_seed)
    other_down = swap_core(sent, sizes)
    grad_active = jnp.dot(grad_seed, down_full.T, preferred_element_type=jnp.float32)
    grad_hidden = (grad_active * slope.astype(jnp.float32)).astype(low)
    grad_down, grad_hidden = tie(grad_down, grad_hidden)
    grad_down = add(core_cut((grad_down,), sizes, 0), other_down)
    sent, grad_hidden = tie(near_cut(grad_down, sizes, 1).astype(low), grad_hidden)
    other_down = swap_near(sent, sizes)
    grad_up = jnp.dot(normed_two.T, grad_hidden, preferred_element_type=jnp.float32)
    grad_hidden, grad_up = tie(grad_hidden, grad_up.astype(low))
    grad_middle, grad_branch, sums_two = matmul_norm_back(
        "mlp_norm_backward", grad_hidden, second, middle, grad_seed, gain_two, 1
    )
    grad_out = jnp.dot(mixed_flat.T, grad_branch, preferred_element_type=jnp.float32).astype(low)
    grad_down, grad_out, other_down = tie(grad_down, grad_out, other_down)
    grad_down = add(near_cut(grad_down, sizes, 0), other_down)
    sent, sent_down, grad_branch = tie(
        core_cut((grad_up, grad_out), sizes, 1), next_cut(grad_down, sizes, 1).astype(low), grad_branch
    )
    other = swap_core(sent, sizes)
    other_down = swap_next(sent_down, sizes)
    grad_mixed = jnp.dot(grad_branch, out_full.T, preferred_element_type=jnp.float32).astype(low)
    grad_up, grad_out, grad_mixed = tie(grad_up, grad_out, grad_mixed)
    upper = add(core_cut((grad_up, grad_out), sizes, 0), other)
    grad_mixed = grad_mixed.reshape(rows_here, length, width)
    sent, grad_mixed = tie(near_cut(upper, sizes, 1).astype(low), grad_mixed)
    other = swap_near(sent, sizes)
    grad_project = jnp.concatenate(
        [
            row_back(project_rows[row], grad_mixed[row], forward[row][1], forward[row][2])
            for row in range(rows_here)
        ],
        axis=0,
    )
    near_far, far_far = (far[1:], far[:1])
    upper, grad_down, grad_project, other, other_down = tie(
        upper, grad_down, grad_project, other, other_down
    )
    grad_qkv = jnp.dot(normed.T, grad_project, preferred_element_type=jnp.float32).astype(low)
    sent, upper, grad_down, grad_project = tie(
        core_cut((grad_qkv,), sizes, 1), upper, grad_down, grad_project
    )
    other_qkv = swap_core(sent, sizes)
    upper = add(near_cut(upper, sizes, 0), other)
    grad_down = add(next_cut(grad_down, sizes, 0), other_down)
    grad_qkv, sent, sent_down = tie(
        grad_qkv,
        next_cut(upper, sizes, 1).astype(low),
        far_cut(grad_down, sizes, near_far, 1).astype(low),
    )
    other = swap_next(sent, sizes)
    other_down = swap_far(sent_down, sizes, near_far)
    grad_qkv = add(core_cut((grad_qkv,), sizes, 0), other_qkv)
    sent, grad_project = tie(near_cut(grad_qkv, sizes, 1).astype(low), grad_project)
    other_qkv = swap_near(sent, sizes)
    grad_tokens, sums_one = matmul_norm_back(
        "attention_norm_backward",
        grad_project,
        first,
        tokens.reshape(rows_here * length, width),
        grad_middle,
        gain_one,
        0,
    )
    grad_tokens = grad_tokens.reshape(rows_here, length, width)
    grad_qkv, sums_one, other_qkv, other, other_down = tie(
        grad_qkv, sums_one, other_qkv, other, other_down
    )
    grad_qkv = add(near_cut(grad_qkv, sizes, 0), other_qkv)
    sent, sums_one, upper, grad_down = tie(
        next_cut(grad_qkv, sizes, 1).astype(low), sums_one, upper, grad_down
    )
    other_qkv = swap_next(sent, sizes)
    upper = add(next_cut(upper, sizes, 0), other)
    grad_down = finish_far(grad_down, other_down, sizes, near_far)
    grad_gain_one, grad_shift_one, grad_gain_two, grad_shift_two = (
        sums_one[0],
        sums_one[1],
        sums_two[0],
        sums_two[1],
    )
    small = jnp.stack([grad_gain_one, grad_shift_one, grad_gain_two, grad_shift_two])
    small = small.reshape(4, shards, piece).transpose(1, 0, 2).reshape(shards, 4 * piece)
    totals = jnp.broadcast_to(jnp.stack([soft, pairs]), (shards, 2))
    small = jnp.concatenate([small, totals], axis=1)
    small = jnp.pad(small, ((0, 0), (0, 128 - small.shape[1])))
    sent_small, sent, sent_down, active = tie(
        core_cut((small,), sizes, 1),
        far_cut(upper, sizes, near_far, 1).astype(low),
        far_cut(grad_down, sizes, far_far, 1).astype(low),
        active,
    )
    other_small = swap_core(sent_small, sizes)
    other = swap_far(sent, sizes, near_far)
    other_down = swap_far(sent_down, sizes, far_far)
    result = middle + jnp.dot(active, down_full, preferred_element_type=jnp.float32)
    output = result.astype(low).reshape(rows_here, length, width)
    grad_qkv, output, other_qkv, other, other_down, other_small = tie(
        grad_qkv, output, other_qkv, other, other_down, other_small
    )
    grad_qkv = add(next_cut(grad_qkv, sizes, 0), other_qkv)
    sent, upper, grad_down, small = tie(
        far_cut(grad_qkv, sizes, near_far, 1).astype(low), upper, grad_down, small
    )
    other_qkv = swap_far(sent, sizes, near_far)
    small = add(core_cut((small,), sizes, 0), other_small)
    other_small = swap_near(near_cut(small, sizes, 1), sizes)
    upper = finish_far(upper, other, sizes, near_far)
    grad_down = finish_far(grad_down, other_down, sizes, far_far)
    upper = scatter_far(upper, sizes, far_far)
    grad_up, grad_out = (upper[:, :wide], upper[:, wide:])
    grad_qkv = finish_far(grad_qkv, other_qkv, sizes, near_far)
    small = add(near_cut(small, sizes, 0), other_small)
    grad_qkv = scatter_far(grad_qkv, sizes, far_far)
    small = add(next_cut(small, sizes, 0), swap_next(next_cut(small, sizes, 1), sizes))
    small = scatter_far(scatter_far(small, sizes, near_far, jnp.float32), sizes, far_far, jnp.float32)[0]
    fraction = small[4 * piece] / small[4 * piece + 1]
    return (
        output,
        grad_tokens,
        grad_qkv,
        grad_out,
        grad_up,
        grad_down,
        small[:piece],
        small[piece : 2 * piece],
        small[2 * piece : 3 * piece],
        small[3 * piece : 4 * piece],
        fraction,
    )


def solution(mesh):
    in_specs = (
        P(("dp", "fsdp"), None, None),
        P(("dp", "fsdp"), None),
        P(("dp", "fsdp")),
        P(("dp", "fsdp"), None),
        P(("dp", "fsdp"), None),
        P(("dp", "fsdp"), None),
        P(("dp", "fsdp"), None),
        P(("dp", "fsdp")),
        P(("dp", "fsdp")),
        P(("dp", "fsdp")),
        P(("dp", "fsdp")),
        P(("dp", "fsdp"), None, None),
    )
    out_specs = (
        P(("dp", "fsdp"), None, None),
        P(("dp", "fsdp"), None, None),
        P(("dp", "fsdp"), None),
        P(("dp", "fsdp"), None),
        P(("dp", "fsdp"), None),
        P(("dp", "fsdp"), None),
        P(("dp", "fsdp")),
        P(("dp", "fsdp")),
        P(("dp", "fsdp")),
        P(("dp", "fsdp")),
        P(),
    )
    return jax.shard_map(
        functools.partial(body, dict(mesh.shape)), mesh=mesh, in_specs=in_specs, out_specs=out_specs, check_vma=False)
```

```python
import functools

import jax
import jax.numpy as jnp
from jax import lax
from jax.experimental import pallas as pl
from jax.experimental.layout import Layout, with_layout_constraint
from jax.experimental.pallas import tpu as pltpu
from jax.sharding import PartitionSpec as P

HEADS = 12
HD = 64


EPSILON = 1e-05
NEGATIVE = -1e30
SOFT_WIDTH = 0.25


def norm_forward(values, gain, shift):
    center = values - jnp.mean(values, axis=-1, keepdims=True)
    spread = jnp.mean(center * center, axis=-1, keepdims=True)
    inverse = lax.rsqrt(spread + EPSILON)
    unit = center * inverse
    return (unit * gain + shift, unit, inverse)


BLOCK = 128
SPAN = 384
NT = (((1,), (1,)), ((), ()))
TN = (((0,), (0,)), ((), ()))


def dot_nt(a, b):
    return lax.dot_general(a, b, NT, preferred_element_type=jnp.float32)


def dot_tn(a, b):
    return lax.dot_general(a, b, TN, preferred_element_type=jnp.float32)


def halves(pair):
    lane = lax.broadcasted_iota(jnp.int32, pair.shape, 1)
    zero = jnp.zeros_like(pair)
    return (jnp.where(lane < HD, pair, zero), jnp.where(lane < HD, zero, pair))


def attend_kernel(limit_ref, seg_ref, project_ref, mixed_ref, lse_ref, bias_ref, stat_ref, column_ref):
    block = pl.program_id(0)
    width = HEADS * HD
    here = pl.multiple_of(block * BLOCK, BLOCK)
    first_key = pl.multiple_of(jnp.maximum(block - 2, 0) * BLOCK, BLOCK)
    rows = pl.ds(here, BLOCK)
    span = pl.ds(first_key, SPAN)

    @pl.when(block == 0)
    def _():
        column_ref[...] = jnp.zeros_like(column_ref)
        stat_ref[...] = jnp.zeros_like(stat_ref)

    low_lane = lax.broadcasted_iota(jnp.int32, (BLOCK, BLOCK), 1)
    bias = None
    for pair in range(HEADS // 2):
        at = pair * 2 * HD
        lanes = slice(at, at + 2 * HD)
        queries = halves(project_ref[rows, lanes] * jnp.bfloat16(HD ** (-0.5)))
        key = project_ref[span, width + at : width + at + 2 * HD]
        value = project_ref[span, 2 * width + at : 2 * width + at + 2 * HD]
        both = dot_nt(key, jnp.concatenate(queries, axis=0))
        outs = []
        for side in range(2):
            head = 2 * pair + side
            scores = both[:, side * BLOCK : (side + 1) * BLOCK]
            if bias is None:
                seg_key = jnp.broadcast_to(seg_ref[:, span], (BLOCK, SPAN)).T
                key_at = first_key + lax.broadcasted_iota(jnp.int32, (SPAN, BLOCK), 0)
                query_at = here + lax.broadcasted_iota(jnp.int32, (SPAN, BLOCK), 1)
                strict = (key_at < query_at) & (seg_ref[:, rows] == seg_key) & (seg_key >= 0)
                allowed = strict | (key_at == query_at)
                select = jnp.where(strict, jnp.maximum(scores, 0.0), 0.0)
                at_row = lax.broadcasted_iota(jnp.int32, (BLOCK, 2 * BLOCK), 0)
                at_lane = lax.broadcasted_iota(jnp.int32, (BLOCK, 2 * BLOCK), 1)
                sums = jnp.dot(
                    select,
                    ((at_row < at_lane) | (at_lane >= BLOCK)).astype(jnp.float32),
                    precision=lax.Precision.HIGHEST,
                    preferred_element_type=jnp.float32,
                )
                before = column_ref[span, :]
                selsum = before + sums[:, :BLOCK]
                column_ref[span, :] = before + sums[:, BLOCK:]
                bias = jnp.where(allowed, -selsum, NEGATIVE)
                bias_ref[...] = bias
                offset = (selsum - limit_ref[0]) * (1.0 / SOFT_WIDTH)
                soft = jnp.where(strict, 1.0 / (1.0 + jnp.exp(-offset)), 0.0)
                stat_ref[0:1, :] += jnp.sum(soft, axis=0, keepdims=True)
                stat_ref[1:2, :] += jnp.sum(jnp.where(strict, 1.0, 0.0), axis=0, keepdims=True)
            logits = scores + bias
            top = jnp.max(logits, axis=0, keepdims=True)
            expo = jnp.exp(logits - top)
            total = jnp.sum(expo, axis=0, keepdims=True)
            probs = (expo * (1.0 / total)).astype(jnp.bfloat16)
            outs.append(dot_tn(probs, value))
            lse_ref[head : head + 1, :] = top + jnp.log(total)
        mixed_ref[:, lanes] = jnp.where(low_lane < HD, outs[0], outs[1]).astype(jnp.bfloat16)


def attend_row(project_row, seg_row, limit):
    length = seg_row.shape[0]
    width = HEADS * HD
    blocks = length // BLOCK
    return pl.pallas_call(
        attend_kernel,
        name="attend_forward",
        grid=(blocks,),
        in_specs=[
            pl.BlockSpec(memory_space=pltpu.SMEM),
            pl.BlockSpec((1, length), lambda i: (0, 0)),
            pl.BlockSpec((length, 3 * width), lambda i: (0, 0), pipeline_mode=pl.Buffered(1)),
        ],
        out_specs=[
            pl.BlockSpec((BLOCK, width), lambda i: (i, 0)),
            pl.BlockSpec((16, BLOCK), lambda i: (0, i)),
            pl.BlockSpec((None, SPAN, BLOCK), lambda i: (i, 0, 0)),
            pl.BlockSpec((8, BLOCK), lambda i: (0, 0)),
        ],
        out_shape=[
            jax.ShapeDtypeStruct((length, width), jnp.bfloat16),
            jax.ShapeDtypeStruct((16, length), jnp.float32),
            jax.ShapeDtypeStruct((blocks, SPAN, BLOCK), jnp.float32),
            jax.ShapeDtypeStruct((8, BLOCK), jnp.float32),
        ],
        scratch_shapes=[pltpu.VMEM((length, BLOCK), jnp.float32)],
        cost_estimate=pl.CostEstimate(
            flops=75 * length * SPAN * width, transcendentals=HEADS * length * SPAN, bytes_accessed=10 * length * width
        ),
    )(limit, seg_row[None], project_row)


def attend_back_kernel(
    project_ref, grad_ref, lse_ref, bias_ref, out_ref, key_ref, value_ref, column_ref, select_ref
):
    block = pl.num_programs(0) - 1 - pl.program_id(0)
    width = HEADS * HD
    here = pl.multiple_of(block * BLOCK, BLOCK)
    first_key = pl.multiple_of(jnp.maximum(block - 2, 0) * BLOCK, BLOCK)
    rows = pl.ds(here, BLOCK)
    span = pl.ds(first_key, SPAN)

    @pl.when(pl.program_id(0) == 0)
    def _():
        key_ref[...] = jnp.zeros_like(key_ref)
        value_ref[...] = jnp.zeros_like(value_ref)
        column_ref[...] = jnp.zeros_like(column_ref)

    bias = jnp.concatenate([bias_ref[...], bias_ref[...]], axis=1)
    for pair in reversed(range(HEADS // 2)):
        at = pair * 2 * HD
        lanes = slice(at, at + 2 * HD)
        queries = halves(project_ref[rows, lanes] * jnp.bfloat16(HD ** (-0.5)))
        queries = jnp.concatenate(queries, axis=0)
        key = project_ref[span, width + at : width + at + 2 * HD]
        value = project_ref[span, 2 * width + at : 2 * width + at + 2 * HD]
        grads = jnp.concatenate(halves(grad_ref[:, lanes]), axis=0)
        lse = jnp.concatenate(
            [lse_ref[2 * pair : 2 * pair + 1, :], lse_ref[2 * pair + 1 : 2 * pair + 2, :]], axis=1
        )
        scores = dot_nt(key, queries)
        probs = jnp.exp(scores + bias - lse)
        grad_probs = dot_nt(value, grads)
        inner = jnp.sum(probs * grad_probs, axis=0, keepdims=True)
        logits_grads = probs * (grad_probs - inner)
        both = logits_grads[:, :BLOCK] + logits_grads[:, BLOCK:]
        if pair == HEADS // 2 - 1:
            select_ref[...] = -both
        else:
            select_ref[...] -= both
        if pair == 0:
            grad_selsum = select_ref[...]
            at_row = lax.broadcasted_iota(jnp.int32, (BLOCK, 2 * BLOCK), 0)
            at_lane = lax.broadcasted_iota(jnp.int32, (BLOCK, 2 * BLOCK), 1)
            after = ((at_row > at_lane) | (at_lane >= BLOCK)).astype(jnp.float32)
            sums = jnp.dot(
                grad_selsum,
                after,
                precision=lax.Precision.HIGHEST,
                preferred_element_type=jnp.float32,
            )
            later = column_ref[span, :]
            grad_select = later + sums[:, :BLOCK]
            column_ref[span, :] = later + sums[:, BLOCK:]
            key_at = first_key + lax.broadcasted_iota(jnp.int32, (SPAN, BLOCK), 0)
            query_at = here + lax.broadcasted_iota(jnp.int32, (SPAN, BLOCK), 1)
            chosen = (bias[:, :BLOCK] > 0.5 * NEGATIVE) & (key_at != query_at)
            chosen = chosen & (scores[:, :BLOCK] > 0.0)
            grad_select = jnp.where(chosen, grad_select, 0.0)
            logits_grads = jnp.concatenate(
                [logits_grads[:, :BLOCK] + grad_select, logits_grads[:, BLOCK:]], axis=1
            )
        low_grads = logits_grads.astype(jnp.bfloat16)
        value_ref[span, lanes] += jnp.dot(
            probs.astype(jnp.bfloat16), grads, preferred_element_type=jnp.float32
        )
        key_ref[span, lanes] += jnp.dot(low_grads, queries, preferred_element_type=jnp.float32)
        query_grad = jnp.dot(key.T, low_grads, preferred_element_type=jnp.float32)
        query_grad = jnp.concatenate([query_grad[:HD, :BLOCK], query_grad[HD:, BLOCK:]], axis=0)
        out_ref[:, lanes] = (query_grad.T * HD ** (-0.5)).astype(jnp.bfloat16)
    out_ref[:, width : 2 * width] = key_ref[rows, :].astype(jnp.bfloat16)
    out_ref[:, 2 * width :] = value_ref[rows, :].astype(jnp.bfloat16)


def row_back(project_row, grad_row, lse_row, bias_row):
    length = project_row.shape[0]
    width = HEADS * HD
    blocks = length // BLOCK
    return pl.pallas_call(
        attend_back_kernel,
        name="attend_backward",
        grid=(blocks,),
        in_specs=[
            pl.BlockSpec((length, 3 * width), lambda i: (0, 0), pipeline_mode=pl.Buffered(1)),
            pl.BlockSpec((BLOCK, width), lambda i: (blocks - 1 - i, 0)),
            pl.BlockSpec((16, BLOCK), lambda i: (0, blocks - 1 - i)),
            pl.BlockSpec((None, SPAN, BLOCK), lambda i: (blocks - 1 - i, 0, 0)),
        ],
        out_specs=pl.BlockSpec((BLOCK, 3 * width), lambda i: (blocks - 1 - i, 0)),
        out_shape=jax.ShapeDtypeStruct((length, 3 * width), jnp.bfloat16),
        scratch_shapes=[
            pltpu.VMEM((length, width), jnp.float32),
            pltpu.VMEM((length, width), jnp.float32),
            pltpu.VMEM((length, BLOCK), jnp.float32),
            pltpu.VMEM((SPAN, BLOCK), jnp.float32),
        ],
        cost_estimate=pl.CostEstimate(
            flops=105 * length * SPAN * width, transcendentals=HEADS * length * SPAN, bytes_accessed=14 * length * width
        ),
    )(project_row, grad_row, lse_row, bias_row)


STRIP = 256


def norm_back_kernel(grad_ref, weight_ref, value_ref, add_ref, gain_ref, out_ref, *rest):
    sums_ref = rest[-1]

    @pl.when(pl.program_id(0) == 0)
    def _():
        sums_ref[...] = jnp.zeros_like(sums_ref)

    grad = dot_nt(grad_ref[...], weight_ref[...])
    value = value_ref[...].astype(jnp.float32)
    center = value - jnp.mean(value, axis=-1, keepdims=True)
    inverse = lax.rsqrt(jnp.mean(center * center, axis=-1, keepdims=True) + EPSILON)
    unit = center * inverse
    sums_ref[0:1, :] += jnp.sum(grad * unit, axis=0, keepdims=True)
    sums_ref[1:2, :] += jnp.sum(grad, axis=0, keepdims=True)
    grad_unit = grad * gain_ref[...]
    centered = grad_unit - jnp.mean(grad_unit, axis=-1, keepdims=True)
    back = inverse * (centered - unit * jnp.mean(grad_unit * unit, axis=-1, keepdims=True))
    total = add_ref[...].astype(jnp.float32) + back
    out_ref[...] = total
    for low_ref in rest[:-1]:
        low_ref[...] = total.astype(jnp.bfloat16)


def matmul_norm_back(name, grad, weight, value, add, gain, low):
    rows, depth = grad.shape
    width = weight.shape[0]
    strip = lambda size: pl.BlockSpec((STRIP, size), lambda i: (i, 0))
    whole = lambda *shape: pl.BlockSpec(shape, lambda i: (0, 0), pipeline_mode=pl.Buffered(1))
    return pl.pallas_call(
        norm_back_kernel,
        name=name,
        grid=(rows // STRIP,),
        in_specs=[strip(depth), whole(width, depth), strip(width), strip(width), whole(1, width)],
        out_specs=[strip(width)] * (1 + low) + [pl.BlockSpec((8, width), lambda i: (0, 0))],
        out_shape=[jax.ShapeDtypeStruct((rows, width), jnp.float32)]
        + [jax.ShapeDtypeStruct((rows, width), jnp.bfloat16)] * low
        + [jax.ShapeDtypeStruct((8, width), jnp.float32)],
        cost_estimate=pl.CostEstimate(
            flops=2 * rows * width * (depth + 3072), transcendentals=rows, bytes_accessed=2 * rows * depth + 2 * width * depth + 14 * rows * width
        ),
    )(grad, weight, value, add, gain[None])


BOTH = ("dp", "fsdp")


def bit_count(sizes):
    return (sizes["dp"] * sizes["fsdp"]).bit_length() - 1


def my_bits(sizes):
    count = bit_count(sizes)
    number = lax.axis_index("dp") * sizes["fsdp"] + lax.axis_index("fsdp")
    return [(number >> (count - 1 - place)) & 1 for place in range(count)]


def exchange(value, sizes, places):
    count = bit_count(sizes)
    masks = [1 << (count - 1 - place) for place in places]
    return lax.ppermute(value, BOTH, [(i, i ^ masks[i & 1]) for i in range(2**count)])


def side_of(shape, axis):
    return lax.broadcasted_iota(jnp.int32, shape, axis)


def join(mine, other, at, bit):
    shape = mine.shape[:at] + (2,) + mine.shape[at:]
    return jnp.where(side_of(shape, at) == bit, jnp.expand_dims(mine, at), jnp.expand_dims(other, at))


def far_places(sizes):
    return list(range(1, bit_count(sizes) - 2))


def gather_far(value, sizes, places):
    bits = my_bits(sizes)
    for place in places:
        value = join(value, exchange(value, sizes, (place, place)), place - 1, bits[place])
    return value


def gather_near(value, sizes):
    bits = my_bits(sizes)
    near = len(bits) - 2
    other = exchange(value, sizes, (0, near))
    return join(value, other, 0, jnp.where(bits[-1] == 0, bits[0], bits[near]))


def gather_last(value, beside, other, sizes):
    bits = my_bits(sizes)
    last = len(bits) - 1
    near = last - 1

    def combine(held, received, even):
        by_first = join(held, received, near, bits[near])
        by_near = join(
            jnp.moveaxis(held, 0, near - 1), jnp.moveaxis(received, 0, near - 1), 0, bits[0]
        )
        return jnp.where(even, by_first, by_near)

    even = bits[last] == 0
    other_beside = swap_core(other, sizes)
    value = join(
        combine(value, other, even), combine(beside, other_beside, jnp.logical_not(even)), last, bits[last]
    )
    return value.reshape((-1,) + value.shape[last + 2 :])


def pick(value, at, bit):
    return lax.dynamic_index_in_dim(value, bit, at, keepdims=False)


def add(mine, other):
    return mine.astype(jnp.float32) + other.astype(jnp.float32)


def core_cut(partials, sizes, flip):
    bits = my_bits(sizes)
    last = len(bits) - 1
    shape = (2,) * len(bits)
    views = [part.reshape(shape + (part.shape[0] >> len(bits),) + part.shape[1:]) for part in partials]
    return jnp.concatenate([pick(view, last, bits[last] ^ flip) for view in views], axis=-1)


def near_cut(value, sizes, flip):
    bits = my_bits(sizes)
    near = len(bits) - 2
    by_near = pick(value, near, bits[near] ^ flip)
    by_first = jnp.moveaxis(pick(value, 0, bits[0] ^ flip), near - 1, 0)
    return jnp.where(bits[-1] == 0, by_near, by_first)


def next_cut(value, sizes, flip):
    bits = my_bits(sizes)
    side = jnp.where(bits[-1] == 0, bits[0], bits[len(bits) - 2])
    return pick(value, 0, side ^ flip)


def swap_core(sent, sizes):
    last = bit_count(sizes) - 1
    return exchange(sent, sizes, (last, last))


def swap_near(sent, sizes):
    return exchange(sent, sizes, (bit_count(sizes) - 2, 0))


def swap_next(sent, sizes):
    return exchange(sent, sizes, (0, bit_count(sizes) - 2))


def far_cut(value, sizes, places, flip):
    place = places[-1]
    return pick(value, place - 1, my_bits(sizes)[place] ^ flip)


def swap_last(value, sizes):
    return exchange(value, sizes, (bit_count(sizes) - 2, 0))


def swap_far(sent, sizes, places):
    return exchange(sent, sizes, (places[-1], places[-1]))


def finish_far(value, other, sizes, places, kind=jnp.bfloat16):
    return scatter_far(add(far_cut(value, sizes, places, 0), other), sizes, places[:-1], kind)


def scatter_far(value, sizes, places, kind=jnp.bfloat16):
    bits = my_bits(sizes)
    for place in reversed(places):
        sent = pick(value, place - 1, 1 - bits[place]).astype(kind)
        value = add(pick(value, place - 1, bits[place]), exchange(sent, sizes, (place, place)))
    return value


def row_major(value):
    return with_layout_constraint(value, Layout(major_to_minor=(0, 1)))


def tie(*values):
    return lax.optimization_barrier(values)


def body(
    sizes,
    tokens,
    segments,
    thresholds,
    qkv_weight,
    out_weight,
    up_weight,
    down_weight,
    attn_gain,
    attn_shift,
    mlp_gain,
    mlp_shift,
    cotangent,
):
    rows_here, length, width = tokens.shape
    shards = sizes["dp"] * sizes["fsdp"]
    piece = width // shards
    small = jnp.stack([attn_gain, attn_shift, mlp_gain, mlp_shift], axis=1)
    small = jnp.pad(small, ((0, 0), (0, 128 - 4)))
    wide = up_weight.shape[1]
    far = far_places(sizes)
    low = jnp.bfloat16
    first = gather_far(jnp.concatenate([qkv_weight, small], axis=1), sizes, far)
    first, up_weight, out_weight = tie(first, up_weight, out_weight)
    first = gather_near(first, sizes)
    second = gather_far(jnp.concatenate([up_weight, out_weight], axis=1), sizes, far[:1])
    first, second = tie(first, second)
    other = swap_last(first, sizes)
    beside = swap_core(first, sizes)
    second = gather_far(second, sizes, far[1:])
    first = row_major(gather_last(first, beside, other, sizes))
    first, second, down_weight = tie(first, second, down_weight)
    second = gather_near(second, sizes)
    down_full = gather_far(down_weight, sizes, far[:1])
    qkv_full = first[:, : 3 * width]
    small = row_major(first[:, 3 * width :])
    small = small[:, :4].astype(jnp.float32).T
    gain_one, shift_one, gain_two, shift_two = (small[0], small[1], small[2], small[3])
    flat = tokens.astype(jnp.float32).reshape(rows_here * length, width)
    normed_float, unit_one, inverse_one = norm_forward(flat, gain_one, shift_one)
    normed = normed_float.astype(jnp.bfloat16)
    project = jnp.dot(normed, qkv_full, preferred_element_type=jnp.float32).astype(jnp.bfloat16)
    project, second, down_full = tie(project, second, down_full)
    other = swap_last(second, sizes)
    beside = swap_core(second, sizes)
    down_full = gather_far(down_full, sizes, far[1:])
    project_rows = project.reshape(rows_here, length, 3 * width)
    forward = [
        attend_row(project_rows[row], segments[row], thresholds[row : row + 1])
        for row in range(rows_here)
    ]
    mixed_flat = jnp.concatenate([item[0] for item in forward], axis=0)
    mixed_flat, other, beside, down_full = tie(mixed_flat, other, beside, down_full)
    second = row_major(gather_last(second, beside, other, sizes))
    up_full, out_full = (second[:, :wide], second[:, wide:])
    down_full = gather_near(down_full, sizes)
    soft = sum(jnp.sum(item[3][0]) for item in forward)
    pairs = sum(jnp.sum(item[3][1]) for item in forward)
    middle = flat + jnp.dot(mixed_flat, out_full, preferred_element_type=jnp.float32)
    normed_two_float, unit_two, inverse_two = norm_forward(middle, gain_two, shift_two)
    normed_two, down_full = tie(normed_two_float.astype(low), down_full)
    other = swap_last(down_full, sizes)
    beside = swap_core(down_full, sizes)
    hidden = jnp.dot(normed_two, up_full, preferred_element_type=jnp.float32)
    squared = hidden * hidden
    curve = jnp.tanh(0.7978845608 * hidden * (1.0 + 0.044715 * squared))
    active = (0.5 * hidden * (1.0 + curve)).astype(low)
    slope = 0.5 * (1.0 + curve) + hidden * (1.0 - curve * curve) * (
        0.3989422804 + 0.0535161226 * squared
    )
    slope = slope.astype(low)
    active, slope, other, beside = tie(active, slope, other, beside)
    down_full = gather_last(down_full, beside, other, sizes)
    grad_seed = jnp.where(
        (segments >= 0)[:, :, None], cotangent, jnp.zeros_like(cotangent)
    ).reshape(rows_here * length, width)
    grad_down = jnp.dot(active.T, grad_seed, preferred_element_type=jnp.float32)
    grad_down = grad_down.astype(low)
    sent, grad_seed = tie(core_cut((grad_down,), sizes, 1), grad_seed)
    other_down = swap_core(sent, sizes)
    grad_active = jnp.dot(grad_seed, down_full.T, preferred_element_type=jnp.float32)
    grad_hidden = (grad_active * slope.astype(jnp.float32)).astype(low)
    grad_down, grad_hidden = tie(grad_down, grad_hidden)
    grad_down = add(core_cut((grad_down,), sizes, 0), other_down)
    sent, grad_hidden = tie(near_cut(grad_down, sizes, 1).astype(low), grad_hidden)
    other_down = swap_near(sent, sizes)
    grad_up = jnp.dot(normed_two.T, grad_hidden, preferred_element_type=jnp.float32)
    grad_hidden, grad_up = tie(grad_hidden, grad_up.astype(low))
    grad_middle, grad_branch, sums_two = matmul_norm_back(
        "mlp_norm_backward", grad_hidden, second, middle, grad_seed, gain_two, 1
    )
    grad_out = jnp.dot(mixed_flat.T, grad_branch, preferred_element_type=jnp.float32).astype(low)
    grad_down, grad_out, other_down = tie(grad_down, grad_out, other_down)
    grad_down = add(near_cut(grad_down, sizes, 0), other_down)
    sent, sent_down, grad_branch = tie(
        core_cut((grad_up, grad_out), sizes, 1), next_cut(grad_down, sizes, 1).astype(low), grad_branch
    )
    other = swap_core(sent, sizes)
    other_down = swap_next(sent_down, sizes)
    grad_mixed = jnp.dot(grad_branch, out_full.T, preferred_element_type=jnp.float32).astype(low)
    grad_up, grad_out, grad_mixed = tie(grad_up, grad_out, grad_mixed)
    upper = add(core_cut((grad_up, grad_out), sizes, 0), other)
    grad_mixed = grad_mixed.reshape(rows_here, length, width)
    sent, grad_mixed = tie(near_cut(upper, sizes, 1).astype(low), grad_mixed)
    other = swap_near(sent, sizes)
    grad_project = jnp.concatenate(
        [
            row_back(project_rows[row], grad_mixed[row], forward[row][1], forward[row][2])
            for row in range(rows_here)
        ],
        axis=0,
    )
    near_far, far_far = (far[1:], far[:1])
    upper, grad_down, grad_project, other, other_down = tie(
        upper, grad_down, grad_project, other, other_down
    )
    upper = add(near_cut(upper, sizes, 0), other)
    sent, grad_project = tie(next_cut(upper, sizes, 1).astype(low), grad_project)
    other = swap_next(sent, sizes)
    grad_qkv = jnp.dot(normed.T, grad_project, preferred_element_type=jnp.float32).astype(low)
    sent, grad_down, grad_project, other = tie(
        core_cut((grad_qkv,), sizes, 1), grad_down, grad_project, other
    )
    other_qkv = swap_core(sent, sizes)
    grad_down = add(next_cut(grad_down, sizes, 0), other_down)
    grad_qkv, sent_down = tie(grad_qkv, far_cut(grad_down, sizes, near_far, 1).astype(low))
    other_down = swap_far(sent_down, sizes, near_far)
    grad_qkv = add(core_cut((grad_qkv,), sizes, 0), other_qkv)
    sent, grad_project = tie(near_cut(grad_qkv, sizes, 1).astype(low), grad_project)
    other_qkv = swap_near(sent, sizes)
    grad_tokens, sums_one = matmul_norm_back(
        "attention_norm_backward",
        grad_project,
        first,
        tokens.reshape(rows_here * length, width),
        grad_middle,
        gain_one,
        0,
    )
    grad_tokens = grad_tokens.reshape(rows_here, length, width)
    grad_qkv, sums_one, other_qkv, other, other_down = tie(
        grad_qkv, sums_one, other_qkv, other, other_down
    )
    grad_qkv = add(near_cut(grad_qkv, sizes, 0), other_qkv)
    sent, sums_one, upper, grad_down = tie(
        next_cut(grad_qkv, sizes, 1).astype(low), sums_one, upper, grad_down
    )
    other_qkv = swap_next(sent, sizes)
    upper = add(next_cut(upper, sizes, 0), other)
    grad_down = finish_far(grad_down, other_down, sizes, near_far)
    grad_gain_one, grad_shift_one, grad_gain_two, grad_shift_two = (
        sums_one[0],
        sums_one[1],
        sums_two[0],
        sums_two[1],
    )
    small = jnp.stack([grad_gain_one, grad_shift_one, grad_gain_two, grad_shift_two])
    small = small.reshape(4, shards, piece).transpose(1, 0, 2).reshape(shards, 4 * piece)
    totals = jnp.broadcast_to(jnp.stack([soft, pairs]), (shards, 2))
    small = jnp.concatenate([small, totals], axis=1)
    small = jnp.pad(small, ((0, 0), (0, 128 - small.shape[1])))
    sent_small, sent, sent_down, active = tie(
        core_cut((small,), sizes, 1),
        far_cut(upper, sizes, near_far, 1).astype(low),
        far_cut(grad_down, sizes, far_far, 1).astype(low),
        active,
    )
    other_small = swap_core(sent_small, sizes)
    other = swap_far(sent, sizes, near_far)
    other_down = swap_far(sent_down, sizes, far_far)
    result = middle + jnp.dot(active, down_full, preferred_element_type=jnp.float32)
    output = result.astype(low).reshape(rows_here, length, width)
    grad_qkv, output, other_qkv, other, other_down, other_small = tie(
        grad_qkv, output, other_qkv, other, other_down, other_small
    )
    grad_qkv = add(next_cut(grad_qkv, sizes, 0), other_qkv)
    sent, upper, grad_down, small = tie(
        far_cut(grad_qkv, sizes, near_far, 1).astype(low), upper, grad_down, small
    )
    other_qkv = swap_far(sent, sizes, near_far)
    small = add(core_cut((small,), sizes, 0), other_small)
    other_small = swap_near(near_cut(small, sizes, 1), sizes)
    upper = finish_far(upper, other, sizes, near_far)
    grad_down = finish_far(grad_down, other_down, sizes, far_far)
    upper = scatter_far(upper, sizes, far_far)
    grad_up, grad_out = (upper[:, :wide], upper[:, wide:])
    grad_qkv = finish_far(grad_qkv, other_qkv, sizes, near_far)
    small = add(near_cut(small, sizes, 0), other_small)
    grad_qkv = scatter_far(grad_qkv, sizes, far_far)
    small = add(next_cut(small, sizes, 0), swap_next(next_cut(small, sizes, 1), sizes))
    small = scatter_far(scatter_far(small, sizes, near_far, jnp.float32), sizes, far_far, jnp.float32)[0]
    fraction = small[4 * piece] / small[4 * piece + 1]
    return (
        output,
        grad_tokens,
        grad_qkv,
        grad_out,
        grad_up,
        grad_down,
        small[:piece],
        small[piece : 2 * piece],
        small[2 * piece : 3 * piece],
        small[3 * piece : 4 * piece],
        fraction,
    )


def solution(mesh):
    in_specs = (
        P(("dp", "fsdp"), None, None),
        P(("dp", "fsdp"), None),
        P(("dp", "fsdp")),
        P(("dp", "fsdp"), None),
        P(("dp", "fsdp"), None),
        P(("dp", "fsdp"), None),
        P(("dp", "fsdp"), None),
        P(("dp", "fsdp")),
        P(("dp", "fsdp")),
        P(("dp", "fsdp")),
        P(("dp", "fsdp")),
        P(("dp", "fsdp"), None, None),
    )
    out_specs = (
        P(("dp", "fsdp"), None, None),
        P(("dp", "fsdp"), None, None),
        P(("dp", "fsdp"), None),
        P(("dp", "fsdp"), None),
        P(("dp", "fsdp"), None),
        P(("dp", "fsdp"), None),
        P(("dp", "fsdp")),
        P(("dp", "fsdp")),
        P(("dp", "fsdp")),
        P(("dp", "fsdp")),
        P(),
    )
    return jax.shard_map(
        functools.partial(body, dict(mesh.shape)), mesh=mesh, in_specs=in_specs, out_specs=out_specs, check_vma=False)
```
